32 devices in a mesh: wide: 8 (over z, x), narrow: 4 (over y, core).
Axes of the slice: x: 2, y: 2, z: 4, core: 2. Of those that a mesh axis runs over, the one named last changes fastest.
Arguments:
- documents: bfloat16 [2048, 768], P('wide'), may hold values from -6 to 6
- weights: bfloat16 [24576, 768], P(('wide', 'narrow')), may hold values from -6 to 6
- momentum: float32 [24576, 768], P(('wide', 'narrow')), may hold values from -6 to 6
- positives: int32 [2048, 8], P('wide'), may hold values from 0 to 24575
- relocation: int32 [24576], replicated, may hold values from 0 to 24575, each once
- pair_docs: int32 [32, 6], replicated, may hold values from -1 to 15, as said below
- pair_labels: int32 [32, 6], replicated, may hold values from 0 to 2
Outputs:
- new_weights: bfloat16 [24576, 768], P(('wide', 'narrow'))
- new_momentum: float32 [24576, 768], P(('wide', 'narrow'))
- doc_grad: float32 [2048, 768], P('wide', 'narrow')
The draws below stay inside these ranges and needn't reach their ends.
Inputs may be any that keep to these rules, and one draw needn't show every extreme that they name: `pair_docs`: row i lists pairs of label blocks i * 3 to i * 3 + 2; live entries come first in each row, then -1, and the live (document block, label block) pairs of a row are distinct. Document block b lies on wide index b // 2. The rows of one run of 4 rows starting at a multiple of 4 name exactly 2 distinct wide indices, one document block of each, and at least one of these rows has no -1.
All inputs are finite; a program needn't handle non-finite values.
Results may differ from the reference program's by a relative error of at most 0.0075.
Values may be sent and summed in bfloat16 or wider, within the bound.
A program may use at most 64 MiB of HBM per device.

```python
import math
import jax
import jax.numpy as jnp
import numpy as np
from jax import lax

D = 768
LBLK = 256
DBLK = 128
LB_DEV = 3
POS = 8
DOC_OWN = 2
FETCH = 2
GROUP_ROWS = 4
LAB_DEV = 768
LABELS = 24576
DOCS = 2048


def order_of(subkey, length):
    return jax.random.permutation(subkey, length).astype(jnp.int32)


def pair_table(key):
    groups = 4 * FETCH
    devices = groups * GROUP_ROWS
    pair_total = FETCH * LB_DEV
    key_owner, key_block, key_order, key_count, key_full = jax.random.split(jax.random.fold_in(key, 11), 5)
    owner_order = jax.vmap(lambda subkey: order_of(subkey, groups))(jax.random.split(key_owner, groups))
    chosen = owner_order[:, :FETCH]
    local_block = jax.random.randint(key_block, (groups, FETCH), 0, DOC_OWN).astype(jnp.int32)
    fetched = chosen * DOC_OWN + local_block
    row_order = jax.vmap(lambda subkey: order_of(subkey, pair_total))(jax.random.split(key_order, devices))
    fetch_pick = (row_order // LB_DEV).astype(jnp.int32)
    label_pick = (row_order % LB_DEV).astype(jnp.int32)
    group_of = (jnp.arange(devices) // GROUP_ROWS).astype(jnp.int32)
    docs_row = jnp.take_along_axis(fetched[group_of], fetch_pick, axis=1)
    lowest = max(1, pair_total // 4)
    live_count = jax.random.randint(key_count, (devices,), lowest, pair_total + 1).astype(jnp.int32)
    full_member = jax.random.randint(key_full, (groups,), 0, GROUP_ROWS).astype(jnp.int32)
    is_full = (jnp.arange(devices) % GROUP_ROWS).astype(jnp.int32) == full_member[group_of]
    live_count = jnp.where(is_full, pair_total, live_count)
    is_live = jnp.arange(pair_total)[None, :] < live_count[:, None]
    return (jnp.where(is_live, docs_row, -1).astype(jnp.int32), label_pick)


def draw_pair_docs(key, part):
    return pair_table(key)[0]


def draw_pair_labels(key, part):
    return pair_table(key)[1]


def plant(array, own_key, least, largest):
    place = [jax.random.randint(jax.random.fold_in(own_key, axis), (), 0, length) for axis, length in enumerate(array.shape)]
    longest = array.shape.index(max(array.shape))
    next_to = place[:longest] + [(place[longest] + 1) % array.shape[longest]] + place[longest + 1:]
    return array.at[tuple(place)].set(least).at[tuple(next_to)].set(largest)


def level_of(stream_key, shape, shards, least, top_value):
    factor_of = 1.0
    for position, shards_of in shards:
        steps = jax.random.uniform(jax.random.fold_in(jax.random.fold_in(stream_key, 6), position), (shards_of,), jnp.float32, least / len(shards), top_value / len(shards))
        factor_of = factor_of * jnp.repeat(jnp.exp(steps), shape[position] // shards_of).reshape((-1,) + (1,) * (len(shape) - 1 - position))
    return factor_of


def rank_bounds(amount, slope):
    loads = [(1 << 20) // math.isqrt(rank ** slope) + 1 for rank in range(1, amount + 1)]
    deviation = 1 + sum(loads) // (1 << 30)
    return np.cumsum(np.array([max(1, weight // deviation) for weight in loads]))


def ranked(rng, shape, number_of, slope):
    table = rank_bounds(number_of, slope)
    lot = jax.random.randint(jax.random.fold_in(rng, 1), shape, 0, int(table[number_of - 1]))
    standing = jnp.searchsorted(jnp.asarray(table, jnp.int32), lot, side="right")
    return jax.random.permutation(jax.random.fold_in(rng, 2), number_of)[standing].astype(jnp.int32)


def gaussian(stream_key, shape, spread, bound, cuts=(), kind=jnp.bfloat16):
    result = jax.random.normal(stream_key, shape, jnp.float32) * spread
    if len(cuts) > 0:
        result = level_of(stream_key, shape, cuts, -0.22, 0.18) * result
    return jnp.clip(result, min=-bound, max=bound).astype(kind)


def setup_inputs(seed: int = 0) -> dict:
    seeds = jax.random.split(jax.random.key(seed), 8)
    documents = gaussian(seeds[0], (DOCS, D), 1.0, 6.0, ((0, 8),))
    weights = gaussian(seeds[1], (LABELS, D), 1.0, 6.0, ((0, 32),))
    momentum = gaussian(seeds[2], (LABELS, D), 1.0, 6.0, ((0, 32),), jnp.float32)
    positives = plant(ranked(seeds[3], (DOCS, POS), LABELS, 2), jax.random.fold_in(seeds[3], 3), 0, LABELS - 1).astype(jnp.int32)
    relocation = jax.random.permutation(seeds[4], LABELS).astype(jnp.int32)
    pair_docs = draw_pair_docs(jax.random.fold_in(seeds[7], 71), 0)
    pair_labels = draw_pair_labels(jax.random.fold_in(seeds[7], 71), 0)
    return {"documents": documents, "weights": weights, "momentum": momentum, "positives": positives, "relocation": relocation, "pair_docs": pair_docs, "pair_labels": pair_labels}


decay_rate = 0.9
step_rate = 0.1

def reference(documents, weights, momentum, positives, relocation, pair_docs, pair_labels):
    logit_scale = 1.0 / math.sqrt(D)
    label_slots = jnp.take(relocation, positives, axis=0)
    row_count = pair_docs.shape[0]
    weight_rows = weights.reshape(row_count, LAB_DEV, D)

    def device_step(grad_docs, inputs):
        local_rows, docs_row, labels_row, device = inputs

        def pair_step(pair_carry, pair_item):

            def live_pair(carried):
                grad_w, grad_x = carried
                doc_start = (pair_item[0] * DBLK).astype(jnp.int32)
                label_start = (pair_item[1] * LBLK).astype(jnp.int32)
                doc_block = lax.dynamic_slice_in_dim(documents, doc_start, DBLK, 0)
                slot_block = lax.dynamic_slice_in_dim(label_slots, doc_start, DBLK, 0)
                label_rows = lax.dynamic_slice_in_dim(local_rows, label_start, LBLK, 0)
                logits = jnp.dot(doc_block, label_rows.T, preferred_element_type=jnp.float32) * logit_scale
                label_ids = (device * LAB_DEV + label_start + jnp.arange(LBLK)).astype(jnp.int32)
                target = jnp.any(slot_block[:, :, None] == label_ids[None, None, :], axis=1).astype(jnp.float32)
                grad_tile = ((jax.nn.sigmoid(logits) - target) * logit_scale).astype(jnp.bfloat16)
                part_w = jnp.dot(grad_tile.T, doc_block, preferred_element_type=jnp.float32)
                part_x = jnp.dot(grad_tile, label_rows, preferred_element_type=jnp.float32)
                grad_w = lax.dynamic_update_slice_in_dim(grad_w, lax.dynamic_slice_in_dim(grad_w, label_start, LBLK, 0) + part_w, label_start, 0)
                grad_x = lax.dynamic_update_slice_in_dim(grad_x, lax.dynamic_slice_in_dim(grad_x, doc_start, DBLK, 0) + part_x, doc_start, 0)
                return (grad_w, grad_x)

            def skip_pair(carried):
                return carried
            return (lax.cond(pair_item[0] >= 0, live_pair, skip_pair, pair_carry), None)
        initial = (jnp.zeros((LAB_DEV, D), jnp.float32), grad_docs)
        (grad_w, grad_docs), _ = lax.scan(pair_step, initial, jnp.stack([docs_row, labels_row], axis=1))
        return (grad_docs, grad_w)
    device_ids = jnp.arange(row_count).astype(jnp.int32)
    doc_grad, weight_grad = lax.scan(device_step, jnp.zeros(documents.shape, jnp.float32), (weight_rows, pair_docs, pair_labels, device_ids))
    weight_grad = weight_grad.reshape(weights.shape)
    new_momentum = decay_rate * momentum + weight_grad
    new_weights = (weights.astype(jnp.float32) - step_rate * new_momentum).astype(jnp.bfloat16)
    return (new_weights, new_momentum, doc_grad)
```

```python
import functools
import math

import jax
import jax.numpy as jnp
from jax import lax
from jax.experimental import pallas as pl
from jax.experimental.pallas import tpu as pltpu
from jax.sharding import PartitionSpec as P

LBLK = 256
DBLK = 128

decay_rate = 0.9
step_rate = 0.1

MESH = pl.DeviceIdType.MESH


def remote(src, dst, send_sem, recv_sem, **axis):
    return pltpu.make_async_remote_copy(
        src_ref=src, dst_ref=dst, send_sem=send_sem, recv_sem=recv_sem,
        device_id=axis, device_id_type=MESH)


def kernel(G, N, F, group_ref, row_docs_ref, row_labels_ref, pos_ref, table_ref, docs_ref, w_hbm,
           grad_ref, x_ref, out_ref,
           w_ref, send_buf, recv_buf, slot_buf, slot_recv, xb, slots, asked_buf,
           gq, rs_recv, ret, ret_recv,
           w_sem, s1, r1, s2, r2, s3, r3, s4, r4, s5, r5):
    g = lax.axis_index("wide")
    n = lax.axis_index("narrow")
    D = docs_ref.shape[1]
    own = docs_ref.shape[0] // DBLK
    part = DBLK // N
    feat = D // N
    labels = w_ref.shape[0]
    lb_dev = labels // LBLK
    pos = pos_ref.shape[0]
    scale = 1.0 / math.sqrt(D)

    w_copy = pltpu.make_async_copy(w_hbm, w_ref, w_sem)
    w_copy.start()

    barrier = pltpu.get_barrier_semaphore()
    for k in range(1, G):
        pl.semaphore_signal(barrier, inc=1, device_id={"wide": lax.rem(g + k, G)}, device_id_type=MESH)
    for k in range(1, N):
        pl.semaphore_signal(barrier, inc=1, device_id={"narrow": lax.rem(n + k, N)}, device_id_type=MESH)

    group = group_ref[...]
    asked = jnp.max(jnp.where((group >= 0) & (group // own == g), group % own, -1), axis=1, keepdims=True)
    asked_buf[...] = jnp.broadcast_to(asked, asked_buf.shape)
    quarter = [docs_ref[pl.ds(pl.multiple_of(b * DBLK + n * part, part), part), :] for b in range(own)]
    for d in range(G):
        pick = quarter[0]
        for b in range(1, own):
            pick = jnp.where(asked[d:d + 1, :] == b, quarter[b], pick)
        send_buf[d] = pick

    mine = group_ref[pl.ds(g, 1), :]
    big = jnp.int32(1 << 30)
    blocks = []
    last = jnp.full((1, 1), -1, jnp.int32)
    for j in range(F):
        last = jnp.min(jnp.where(mine > last, mine, big), axis=1, keepdims=True)
        blocks.append(last)

    pl.semaphore_wait(barrier, G - 1 + N - 1)

    wide_copies = []
    for k in range(1, G):
        to = lax.rem(g + k, G)
        copy = remote(send_buf.at[to], recv_buf.at[g], s1.at[k], r1.at[k], wide=to)
        copy.start()
        wide_copies.append(copy)

    table = table_ref[...]
    height = table.shape[0]
    pieces = []
    top = height * 128 - 1
    shift = 0
    while (top >> shift) > 0:
        pieces.append(((table >> shift) & 255).astype(jnp.float32).astype(jnp.bfloat16))
        shift += 8
    n_docs = docs_ref.shape[0]
    hi_iota = lax.broadcasted_iota(jnp.int32, (height, n_docs), 0)
    lo_iota = lax.broadcasted_iota(jnp.int32, (128, n_docs), 0)
    for p in range(pos):
        ids = pos_ref[p:p + 1, :]
        hot = jnp.where(hi_iota == ids // 128, 1.0, 0.0).astype(jnp.bfloat16)
        low = lo_iota == ids % 128
        total = jnp.zeros((1, n_docs), jnp.float32)
        for i, piece in enumerate(pieces):
            rows = lax.dot_general(piece, hot, (((0,), (0,)), ((), ())), preferred_element_type=jnp.float32)
            total = total + jnp.sum(jnp.where(low, rows, 0.0), axis=0, keepdims=True) * float(1 << (8 * i))
        slot_buf[p:p + 1, :] = total.astype(jnp.int32)

    slot_recv[g] = slot_buf[...]
    recv_buf[g] = send_buf[g]
    for k in range(1, G):
        to = lax.rem(g + k, G)
        copy = remote(slot_buf, slot_recv.at[g], s2.at[k], r2.at[k], wide=to)
        copy.start()
        wide_copies.append(copy)
    for copy in wide_copies:
        copy.wait_recv()

    for j in range(F):
        owner = blocks[j] // own
        local = blocks[j] % own
        pick = recv_buf[0]
        spick = slot_recv[0]
        for s in range(1, G):
            pick = jnp.where(owner == s, recv_buf[s], pick)
            spick = jnp.where(owner == s, slot_recv[s], spick)
        xb[j, n] = pick
        chosen = spick[:, :DBLK]
        for b in range(1, own):
            chosen = jnp.where(local == b, spick[:, b * DBLK:(b + 1) * DBLK], chosen)
        slots[:, j * DBLK:(j + 1) * DBLK] = chosen

    narrow_copies = []
    for k in range(1, N):
        to = lax.rem(n + k, N)
        copy = remote(xb.at[:, n], xb.at[:, n], s3.at[k], r3.at[k], narrow=to)
        copy.start()
        narrow_copies.append(copy)

    w_copy.wait()
    for copy in narrow_copies:
        copy.wait_recv()

    row_docs = row_docs_ref[pl.ds(g * N + n, 1), :]
    row_labels = row_labels_ref[pl.ds(g * N + n, 1), :]
    label_base = (g * N + n) * labels
    step = 2 if F % 2 == 0 else 1
    width = step * DBLK
    lane_block = lax.broadcasted_iota(jnp.int32, (1, width), 1) // DBLK
    for j0 in range(0, F, step):
        x = xb[j0:j0 + step].reshape(width, D)
        x_ref[j0 * DBLK:j0 * DBLK + width, :] = x
        chosen_slots = slots[:, j0 * DBLK:j0 * DBLK + width]
        for c in range(lb_dev):
            weight = jnp.zeros((1, width), jnp.float32)
            for jj in range(step):
                live = jnp.max(
                    jnp.where((row_docs == blocks[j0 + jj]) & (row_labels == c), 1.0, 0.0),
                    axis=1, keepdims=True)
                weight = jnp.where(lane_block == jj, live, weight)
            logits = lax.dot_general(
                w_ref[c * LBLK:(c + 1) * LBLK, :], x, (((1,), (1,)), ((), ())),
                preferred_element_type=jnp.float32) * scale
            ids = lax.broadcasted_iota(jnp.int32, (LBLK, width), 0) + (label_base + c * LBLK)
            hit = ids == chosen_slots[0:1, :]
            for p in range(1, pos):
                hit = hit | (ids == chosen_slots[p:p + 1, :])
            target = jnp.where(hit, 1.0, 0.0)
            grad = ((jax.nn.sigmoid(logits) - target) * scale * weight).astype(jnp.bfloat16)
            grad_ref[c * LBLK:(c + 1) * LBLK, j0 * DBLK:j0 * DBLK + width] = grad
        tile = grad_ref[:, j0 * DBLK:j0 * DBLK + width]
        gx = lax.dot_general(w_ref[...], tile, (((0,), (0,)), ((), ())), preferred_element_type=jnp.float32)
        gq[:, :, j0 * DBLK:j0 * DBLK + width] = gx.astype(jnp.bfloat16).reshape(N, feat, width)

    rs_copies = []
    for k in range(1, N):
        to = lax.rem(n + k, N)
        copy = remote(gq.at[to], rs_recv.at[n], s4.at[k], r4.at[k], narrow=to)
        copy.start()
        rs_copies.append(copy)
    for copy in rs_copies:
        copy.wait_recv()
    total = gq[n].astype(jnp.float32)
    for k in range(1, N):
        total = total + rs_recv[lax.rem(n + k, N)].astype(jnp.float32)
    for d in range(G):
        back = jnp.zeros((feat, DBLK), jnp.float32)
        for j in range(F):
            back = jnp.where(blocks[j] // own == d, total[:, j * DBLK:(j + 1) * DBLK], back)
        ret[d] = back.astype(jnp.bfloat16)

    ret_copies = []
    for k in range(1, G):
        to = lax.rem(g + k, G)
        copy = remote(ret.at[to], ret_recv.at[g], s5.at[k], r5.at[k], wide=to)
        copy.start()
        ret_copies.append(copy)
    ret_recv[g] = ret[g]
    for copy in ret_copies:
        copy.wait_recv()
    sums = [jnp.zeros((feat, DBLK), jnp.float32) for _ in range(own)]
    for s in range(G):
        value = ret_recv[s].astype(jnp.float32)
        who = asked_buf[s:s + 1, :]
        for b in range(own):
            sums[b] = sums[b] + jnp.where(who == b, value, 0.0)
    for b in range(own):
        out_ref[:, b * DBLK:(b + 1) * DBLK] = sums[b]

    for copy in wide_copies + narrow_copies + rs_copies + ret_copies:
        copy.wait_send()


def per_device(documents, weights, momentum, positives, relocation, pair_docs, pair_labels):
    G = lax.axis_size("wide")
    N = lax.axis_size("narrow")
    labels, D = weights.shape
    lb_dev = labels // LBLK
    F = pair_docs.shape[1] // lb_dev
    docs = documents.shape[0]
    feat = D // N
    part = DBLK // N
    pos = positives.shape[1]
    group = pair_docs.reshape(G, -1)
    table = relocation.reshape(-1, 128)
    vmem = pl.BlockSpec(memory_space=pltpu.VMEM)
    dma = pltpu.SemaphoreType.DMA
    bf16 = jnp.bfloat16
    grad, x, out = pl.pallas_call(
        functools.partial(kernel, G, N, F),
        out_shape=(
            jax.ShapeDtypeStruct((labels, F * DBLK), bf16),
            jax.ShapeDtypeStruct((F * DBLK, D), bf16),
            jax.ShapeDtypeStruct((feat, docs), jnp.float32),
        ),
        in_specs=[vmem] * 6 + [pl.BlockSpec(memory_space=pl.ANY)],
        out_specs=(vmem, vmem, vmem),
        scratch_shapes=[
            pltpu.VMEM((labels, D), bf16),
            pltpu.VMEM((G, part, D), bf16),
            pltpu.VMEM((G, part, D), bf16),
            pltpu.VMEM((pos, docs), jnp.int32),
            pltpu.VMEM((G, pos, docs), jnp.int32),
            pltpu.VMEM((F, N, part, D), bf16),
            pltpu.VMEM((pos, F * DBLK), jnp.int32),
            pltpu.VMEM((G, 128), jnp.int32),
            pltpu.VMEM((N, feat, F * DBLK), bf16),
            pltpu.VMEM((N, feat, F * DBLK), bf16),
            pltpu.VMEM((G, feat, DBLK), bf16),
            pltpu.VMEM((G, feat, DBLK), bf16),
            dma,
            dma((G,)), dma((G,)), dma((G,)), dma((G,)),
            dma((N,)), dma((N,)), dma((N,)), dma((N,)),
            dma((G,)), dma((G,)),
        ],
        compiler_params=pltpu.CompilerParams(
            collective_id=0, has_side_effects=True, vmem_limit_bytes=48 << 20),
    )(group, pair_docs, pair_labels, positives.T, table, documents, weights)
    grad_w = jnp.dot(grad, x, preferred_element_type=jnp.float32)
    new_momentum = decay_rate * momentum + grad_w
    new_weights = (weights.astype(jnp.float32) - step_rate * new_momentum).astype(jnp.bfloat16)
    return (new_weights, new_momentum, out.T)


def solution(mesh):
    in_specs = (
        P("wide", None),
        P(("wide", "narrow"), None),
        P(("wide", "narrow"), None),
        P("wide", None),
        P(),
        P(),
        P(),
    )
    out_specs = (P(("wide", "narrow"), None), P(("wide", "narrow"), None), P("wide", "narrow"))
    return jax.shard_map(
        per_device, mesh=mesh, in_specs=in_specs, out_specs=out_specs, check_vma=False
    )
```

```python
import functools
import math

import jax
import jax.numpy as jnp
from jax import lax
from jax.experimental import pallas as pl
from jax.experimental.pallas import tpu as pltpu
from jax.sharding import PartitionSpec as P

LBLK = 256
DBLK = 128
CHUNKS = 2

decay_rate = 0.9
step_rate = 0.1

MESH = pl.DeviceIdType.MESH


def remote(src, dst, send_sem, recv_sem, **axis):
    return pltpu.make_async_remote_copy(
        src_ref=src, dst_ref=dst, send_sem=send_sem, recv_sem=recv_sem,
        device_id=axis, device_id_type=MESH)


def kernel(G, N, F, docs_hbm, pos_hbm, table_hbm, pd_hbm, pl_hbm, w_hbm, m_hbm,
           new_w_ref, new_m_ref, out_ref,
           docs_ref, pos_ref, table_ref, pd_ref, pl_ref, w_ref,
           send_buf, recv_buf, slot_buf, slot_recv, xb, slots, asked_buf, grad_ref,
           gq, rs1, mid, rs2, ret, ret_recv,
           in_sem, ws, wr, ss, sr, as_, ar, bs, br, cs, cr, ds_, dr, es, er, fs, fr):
    g = lax.axis_index("wide")
    n = lax.axis_index("narrow")
    D = docs_ref.shape[1]
    own = docs_ref.shape[0] // DBLK
    half = DBLK // CHUNKS
    part = half // N
    feat = D // N
    labels = w_ref.shape[0]
    lb_dev = labels // LBLK
    pos = pos_ref.shape[0]
    scale = 1.0 / math.sqrt(D)
    outer = N // 2
    partner = n + 1 - 2 * (n % 2)
    sent = []

    barrier = pltpu.get_barrier_semaphore()
    for k in range(1, G):
        pl.semaphore_signal(barrier, inc=1, device_id={"wide": lax.rem(g + k, G)}, device_id_type=MESH)
    for k in range(1, N):
        pl.semaphore_signal(barrier, inc=1, device_id={"narrow": lax.rem(n + k, N)}, device_id_type=MESH)

    loads = [
        pltpu.make_async_copy(src, dst, in_sem.at[i])
        for i, (src, dst) in enumerate((
            (pd_hbm, pd_ref), (pl_hbm, pl_ref), (docs_hbm, docs_ref), (pos_hbm, pos_ref),
            (table_hbm, table_ref), (w_hbm, w_ref), (m_hbm, new_m_ref)))
    ]
    for load in loads:
        load.start()
    loads[0].wait()
    loads[1].wait()

    pair_docs = pd_ref[...]
    pair_labels = pl_ref[...]
    device_of = lax.broadcasted_iota(jnp.int32, pair_docs.shape, 1)
    group_of = device_of // N
    local = jnp.where((pair_docs >= 0) & (pair_docs // own == g), pair_docs % own, -1)

    def least(x):
        return jnp.min(jnp.min(x, axis=0, keepdims=True), axis=1, keepdims=True)

    def largest(x):
        return jnp.max(jnp.max(x, axis=0, keepdims=True), axis=1, keepdims=True)

    asked = [largest(jnp.where(group_of == d, local, -1)) for d in range(G)]
    big = jnp.int32(1 << 30)
    mine = jnp.where(group_of == g, pair_docs, -1)
    blocks = []
    last = jnp.full((1, 1), -1, jnp.int32)
    for j in range(F):
        last = least(jnp.where(mine > last, mine, big))
        blocks.append(last)
    owner = [b // own for b in blocks]

    loads[2].wait()
    for h in range(CHUNKS):
        rows = [
            docs_ref[pl.ds(pl.multiple_of(b * DBLK + h * half + n * part, part), part), :]
            for b in range(own)]
        for d in range(G):
            pick = rows[0]
            for b in range(1, own):
                pick = jnp.where(asked[d] == b, rows[b], pick)
            send_buf[h, d] = pick
    for d in range(G):
        asked_buf[d:d + 1, :] = jnp.broadcast_to(asked[d], (1, asked_buf.shape[1]))

    loads[3].wait()
    loads[4].wait()
    table = table_ref[...]
    height = table.shape[0]
    pieces = []
    shift = 0
    while ((height * 128 - 1) >> shift) > 0:
        pieces.append(((table >> shift) & 255).astype(jnp.float32).astype(jnp.bfloat16))
        shift += 8
    n_docs = docs_ref.shape[0]
    hi_iota = lax.broadcasted_iota(jnp.int32, (height, n_docs), 0)
    lo_iota = lax.broadcasted_iota(jnp.int32, (128, n_docs), 0)
    for p in range(pos):
        ids = pos_ref[p:p + 1, :]
        hot = jnp.where(hi_iota == ids // 128, 1.0, 0.0).astype(jnp.bfloat16)
        low = lo_iota == ids % 128
        total = jnp.zeros((1, n_docs), jnp.float32)
        for i, piece in enumerate(pieces):
            rows = lax.dot_general(piece, hot, (((0,), (0,)), ((), ())), preferred_element_type=jnp.float32)
            total = total + jnp.sum(jnp.where(low, rows, 0.0), axis=0, keepdims=True) * float(1 << (8 * i))
        slot_buf[p:p + 1, :] = total.astype(jnp.int32)

    pl.semaphore_wait(barrier, G - 1 + N - 1)

    slot_copies = []
    for k in range(1, G):
        to = lax.rem(g + k, G)
        copy = remote(slot_buf, slot_recv.at[g], ss.at[k], sr.at[k], wide=to)
        copy.start()
        slot_copies.append(copy)
    wide_copies = []
    for h in range(CHUNKS):
        copies = []
        for k in range(1, G):
            to = lax.rem(g + k, G)
            copy = remote(send_buf.at[h, to], recv_buf.at[h, g], ws.at[h, k], wr.at[h, k], wide=to)
            copy.start()
            copies.append(copy)
        wide_copies.append(copies)
        sent.extend(copies)
    sent.extend(slot_copies)
    slot_recv[g] = slot_buf[...]
    for h in range(CHUNKS):
        recv_buf[h, g] = send_buf[h, g]

    def take_wide(h):
        for copy in wide_copies[h]:
            copy.wait_recv()
        for j in range(F):
            pick = recv_buf[h, 0]
            for s in range(1, G):
                pick = jnp.where(owner[j] == s, recv_buf[h, s], pick)
            xb[h, j, n] = pick

    def take_slots():
        for copy in slot_copies:
            copy.wait_recv()
        for j in range(F):
            spick = slot_recv[0]
            for s in range(1, G):
                spick = jnp.where(owner[j] == s, slot_recv[s], spick)
            chosen = spick[:, :DBLK]
            for b in range(1, own):
                chosen = jnp.where(blocks[j] % own == b, spick[:, b * DBLK:(b + 1) * DBLK], chosen)
            for h in range(CHUNKS):
                slots[h, :, j * half:(j + 1) * half] = chosen[:, h * half:(h + 1) * half]

    def gather_send(h):
        piece = xb.at[h, :, n]
        across = []
        for k in range(1, outer):
            copy = remote(piece, piece, bs.at[h, k], br.at[h, k], narrow=lax.rem(n + 2 * k, N))
            copy.start()
            across.append(copy)
        near = remote(piece, piece, as_.at[h], ar.at[h], narrow=partner)
        near.start()
        sent.extend(across + [near])
        return across, near

    def gather_forward(h, across):
        passed = []
        for k in range(1, outer):
            across[k - 1].wait_recv()
            piece = xb.at[h, :, lax.rem(n + N - 2 * k, N)]
            copy = remote(piece, piece, cs.at[h, k], cr.at[h, k], narrow=partner)
            copy.start()
            passed.append(copy)
        sent.extend(passed)
        return passed

    me = g * N + n
    label_base = me * labels
    step = 4 if F % 4 == 0 else 2 if F % 2 == 0 else 1
    width = step * half
    span = F * half
    lane_block = lax.broadcasted_iota(jnp.int32, (1, width), 1) // half
    live = [[
        largest(jnp.where((pair_docs == blocks[j]) & (pair_labels == c) & (device_of == me), 1.0, 0.0))
        for c in range(lb_dev)] for j in range(F)]

    def compute(h):
        for j0 in range(0, F, step):
            x = xb[h, j0:j0 + step].reshape(width, D)
            at = h * span + j0 * half
            chosen_slots = slots[h, :, j0 * half:j0 * half + width]
            for c in range(lb_dev):
                weight = live[j0][c]
                for jj in range(1, step):
                    weight = jnp.where(lane_block == jj, live[j0 + jj][c], weight)
                logits = lax.dot_general(
                    w_ref[c * LBLK:(c + 1) * LBLK, :], x, (((1,), (1,)), ((), ())),
                    preferred_element_type=jnp.float32) * scale
                ids = lax.broadcasted_iota(jnp.int32, (LBLK, width), 0) + (label_base + c * LBLK)
                hit = ids == chosen_slots[0:1, :]
                for p in range(1, pos):
                    hit = hit | (ids == chosen_slots[p:p + 1, :])
                target = jnp.where(hit, 1.0, 0.0)
                grad = ((jax.nn.sigmoid(logits) - target) * scale * weight).astype(jnp.bfloat16)
                grad_ref[c * LBLK:(c + 1) * LBLK, at:at + width] = grad
            gx = lax.dot_general(
                w_ref[...], grad_ref[:, at:at + width], (((0,), (0,)), ((), ())),
                preferred_element_type=jnp.float32)
            gq[h, :, :, j0 * half:j0 * half + width] = gx.astype(jnp.bfloat16).reshape(N, feat, width)

    def reduce_first(h):
        copies = []
        for k in reversed(range(outer)):
            copy = remote(gq.at[h, lax.rem(partner + 2 * k, N)], rs1.at[h, k], ds_.at[h, k], dr.at[h, k],
                          narrow=partner)
            copy.start()
            copies.append(copy)
        sent.extend(copies)
        return copies[::-1]

    def reduce_second(h, first):
        copies = []
        for k in range(1, outer):
            first[k].wait_recv()
            to = lax.rem(n + 2 * k, N)
            mid[h, k] = (gq[h, to].astype(jnp.float32) + rs1[h, k].astype(jnp.float32)).astype(jnp.bfloat16)
            copy = remote(mid.at[h, k], rs2.at[h, k], es.at[h, k], er.at[h, k], narrow=to)
            copy.start()
            copies.append(copy)
        sent.extend(copies)
        return copies

    def send_back(h, first, second):
        first[0].wait_recv()
        total = gq[h, n].astype(jnp.float32) + rs1[h, 0].astype(jnp.float32)
        for k in range(1, outer):
            second[k - 1].wait_recv()
            total = total + rs2[h, k].astype(jnp.float32)
        total = total.astype(jnp.bfloat16)
        rows = feat // CHUNKS
        packed = [
            jnp.concatenate(
                [total[i * rows:(i + 1) * rows, j * half:(j + 1) * half] for i in range(CHUNKS)], axis=1)
            for j in range(F)]
        for d in range(G):
            back = jnp.zeros((rows, DBLK), jnp.bfloat16)
            for j in range(F):
                back = jnp.where(owner[j] == d, packed[j], back)
            ret[h, d] = back
        copies = []
        for k in range(1, G):
            to = lax.rem(g + k, G)
            copy = remote(ret.at[h, to], ret_recv.at[h, g], fs.at[h, k], fr.at[h, k], wide=to)
            copy.start()
            copies.append(copy)
        ret_recv[h, g] = ret[h, g]
        sent.extend(copies)
        return copies

    def update(c):
        rows = slice(c * LBLK, (c + 1) * LBLK)
        grad_w = jnp.dot(
            grad_ref[rows, :], xb[...].reshape(CHUNKS * span, D), preferred_element_type=jnp.float32)
        momentum = decay_rate * new_m_ref[rows, :] + grad_w
        new_m_ref[rows, :] = momentum
        new_w_ref[rows, :] = (w_ref[rows, :].astype(jnp.float32) - step_rate * momentum).astype(jnp.bfloat16)

    def take_back(h, copies):
        for copy in copies:
            copy.wait_recv()
        rows = feat // CHUNKS
        for b in range(own):
            total = jnp.zeros((rows, DBLK), jnp.float32)
            for s in range(G):
                total = total + jnp.where(asked_buf[s:s + 1, :] == b, ret_recv[h, s].astype(jnp.float32), 0.0)
            for i in range(CHUNKS):
                out_ref[i * rows:(i + 1) * rows, b * DBLK + h * half:b * DBLK + (h + 1) * half] = (
                    total[:, i * half:(i + 1) * half])

    take_slots()
    gathers = []
    for h in range(CHUNKS):
        take_wide(h)
        across, near = gather_send(h)
        if h + 1 < CHUNKS:
            passed = gather_forward(h, across)
        else:
            passed = None
        gathers.append([across, near, passed])
    loads[5].wait()

    backs = []
    pending = None
    for h in range(CHUNKS):
        across, near, passed = gathers[h]
        if passed is None:
            passed = gather_forward(h, across)
        if pending is not None:
            pending = pending + (reduce_second(pending[0], pending[1]),)
        near.wait_recv()
        for copy in passed:
            copy.wait_recv()
        compute(h)
        first = reduce_first(h)
        if pending is not None:
            backs.append(send_back(*pending))
        pending = (h, first)
    loads[6].wait()
    update(0)
    pending = pending + (reduce_second(*pending),)
    for c in range(1, lb_dev - 1):
        update(c)
    backs.append(send_back(*pending))
    for c in range(max(1, lb_dev - 1), lb_dev):
        update(c)
    for h in range(CHUNKS):
        take_back(h, backs[h])

    for copy in sent:
        copy.wait_send()


def per_device(documents, weights, momentum, positives, relocation, pair_docs, pair_labels):
    G = lax.axis_size("wide")
    N = lax.axis_size("narrow")
    labels, D = weights.shape
    lb_dev = labels // LBLK
    F = pair_docs.shape[1] // lb_dev
    docs = documents.shape[0]
    feat = D // N
    half = DBLK // CHUNKS
    part = half // N
    pos = positives.shape[1]
    outer = N // 2
    span = F * half
    table = relocation.reshape(-1, 128)
    pair_docs = pair_docs.T
    pair_labels = pair_labels.T
    positives = positives.T
    vmem = pl.BlockSpec(memory_space=pltpu.VMEM)
    hbm = pl.BlockSpec(memory_space=pltpu.HBM)
    dma = pltpu.SemaphoreType.DMA
    bf16 = jnp.bfloat16
    f32 = jnp.float32
    C = CHUNKS
    new_weights, new_momentum, out = pl.pallas_call(
        functools.partial(kernel, G, N, F),
        out_shape=(
            jax.ShapeDtypeStruct((labels, D), bf16),
            jax.ShapeDtypeStruct((labels, D), f32),
            jax.ShapeDtypeStruct((feat, docs), f32),
        ),
        in_specs=[hbm] * 7,
        out_specs=(vmem, vmem, vmem),
        scratch_shapes=[
            pltpu.VMEM(documents.shape, bf16),
            pltpu.VMEM(positives.shape, jnp.int32),
            pltpu.VMEM(table.shape, jnp.int32),
            pltpu.VMEM(pair_docs.shape, jnp.int32),
            pltpu.VMEM(pair_labels.shape, jnp.int32),
            pltpu.VMEM((labels, D), bf16),
            pltpu.VMEM((C, G, part, D), bf16),
            pltpu.VMEM((C, G, part, D), bf16),
            pltpu.VMEM((pos, docs), jnp.int32),
            pltpu.VMEM((G, pos, docs), jnp.int32),
            pltpu.VMEM((C, F, N, part, D), bf16),
            pltpu.VMEM((C, pos, span), jnp.int32),
            pltpu.VMEM((G, 128), jnp.int32),
            pltpu.VMEM((labels, C * span), bf16),
            pltpu.VMEM((C, N, feat, span), bf16),
            pltpu.VMEM((C, outer, feat, span), bf16),
            pltpu.VMEM((C, outer, feat, span), bf16),
            pltpu.VMEM((C, outer, feat, span), bf16),
            pltpu.VMEM((C, G, feat // C, DBLK), bf16),
            pltpu.VMEM((C, G, feat // C, DBLK), bf16),
            dma((7,)),
            dma((C, G)), dma((C, G)), dma((G,)), dma((G,)),
            dma((C,)), dma((C,)), dma((C, outer)), dma((C, outer)), dma((C, outer)), dma((C, outer)),
            dma((C, outer)), dma((C, outer)), dma((C, outer)), dma((C, outer)),
            dma((C, G)), dma((C, G)),
        ],
        compiler_params=pltpu.CompilerParams(
            collective_id=0, has_side_effects=True, vmem_limit_bytes=48 << 20),
    )(*(pltpu.with_memory_space_constraint(x, pltpu.HBM) for x in (
        documents, positives, table, pair_docs, pair_labels, weights, momentum)))
    return (new_weights, new_momentum, out.T)


def solution(mesh):
    in_specs = (
        P("wide", None),
        P(("wide", "narrow"), None),
        P(("wide", "narrow"), None),
        P("wide", None),
        P(),
        P(),
        P(),
    )
    out_specs = (P(("wide", "narrow"), None), P(("wide", "narrow"), None), P("wide", "narrow"))
    return jax.shard_map(
        per_device, mesh=mesh, in_specs=in_specs, out_specs=out_specs, check_vma=False
    )
```

```python
import functools
import math

import jax
import jax.numpy as jnp
from jax import lax
from jax.experimental import pallas as pl
from jax.experimental.pallas import tpu as pltpu
from jax.sharding import PartitionSpec as P

LBLK = 256
DBLK = 128
CHUNKS = 2

decay_rate = 0.9
step_rate = 0.1

MESH = pl.DeviceIdType.MESH


def remote(src, dst, send_sem, recv_sem, **axis):
    return pltpu.make_async_remote_copy(
        src_ref=src, dst_ref=dst, send_sem=send_sem, recv_sem=recv_sem,
        device_id=axis, device_id_type=MESH)


def peers(g, G):
    if G & (G - 1):
        return [lax.rem(g + k, G) for k in range(1, G)]
    order = []
    for m in list(range(G // 2, G)) + list(range(1, G // 2)):
        to = g
        for b in range(G.bit_length() - 1):
            if m >> b & 1:
                to = to + (1 - 2 * ((g // (1 << b)) % 2)) * (1 << b)
        order.append(to)
    return order


def kernel(G, N, F, docs_hbm, pos_hbm, table_hbm, pd_hbm, pl_hbm, w_hbm, m_hbm,
           new_w_ref, new_m_ref, out_ref,
           docs_ref, pos_ref, table_ref, pd_ref, pl_ref, w_ref,
           send_buf, recv_buf, slot_buf, slot_recv, xb, slots, asked_buf, grad_ref,
           gq, rs1, mid, rs2, ret, ret_recv,
           in_sem, ws, wr, ss, sr, as_, ar, bs, br, cs, cr, ds_, dr, es, er, fs, fr):
    g = lax.axis_index("wide")
    n = lax.axis_index("narrow")
    D = docs_ref.shape[1]
    own = docs_ref.shape[0] // DBLK
    half = DBLK // CHUNKS
    part = half // N
    feat = D // N
    labels = w_ref.shape[0]
    lb_dev = labels // LBLK
    pos = pos_ref.shape[0]
    scale = 1.0 / math.sqrt(D)
    outer = N // 2
    partner = n + 1 - 2 * (n % 2)
    sent = []

    order = list(enumerate(peers(g, G), 1))
    barrier = pltpu.get_barrier_semaphore()
    for k, to in order:
        pl.semaphore_signal(barrier, inc=1, device_id={"wide": to}, device_id_type=MESH)
    for k in range(1, N):
        pl.semaphore_signal(barrier, inc=1, device_id={"narrow": lax.rem(n + k, N)}, device_id_type=MESH)

    loads = [
        pltpu.make_async_copy(src, dst, in_sem.at[i])
        for i, (src, dst) in enumerate((
            (pd_hbm, pd_ref), (docs_hbm, docs_ref), (pl_hbm, pl_ref), (pos_hbm, pos_ref),
            (table_hbm, table_ref), (w_hbm, w_ref), (m_hbm, new_m_ref)))
    ]
    for load in loads:
        load.start()
    loads[0].wait()

    pair_docs = pd_ref[...]
    device_of = lax.broadcasted_iota(jnp.int32, pair_docs.shape, 1)
    group_of = device_of // N
    local = jnp.where((pair_docs >= 0) & (pair_docs // own == g), pair_docs % own, -1)

    def least(x):
        return jnp.min(jnp.min(x, axis=0, keepdims=True), axis=1, keepdims=True)

    def largest(x):
        return jnp.max(jnp.max(x, axis=0, keepdims=True), axis=1, keepdims=True)

    asked = [largest(jnp.where(group_of == d, local, -1)) for d in range(G)]
    big = jnp.int32(1 << 30)
    mine = jnp.where(group_of == g, pair_docs, -1)
    blocks = []
    last = jnp.full((1, 1), -1, jnp.int32)
    for j in range(F):
        last = least(jnp.where(mine > last, mine, big))
        blocks.append(last)
    owner = [b // own for b in blocks]

    loads[1].wait()
    for h in range(CHUNKS):
        rows = [
            docs_ref[pl.ds(pl.multiple_of(b * DBLK + h * half + n * part, part), part), :]
            for b in range(own)]
        for d in range(G):
            pick = rows[0]
            for b in range(1, own):
                pick = jnp.where(asked[d] == b, rows[b], pick)
            send_buf[h, d] = pick
    for d in range(G):
        asked_buf[d:d + 1, :] = jnp.broadcast_to(asked[d], (1, asked_buf.shape[1]))

    pl.semaphore_wait(barrier, G - 1 + N - 1)

    wide_copies = []
    for h in range(CHUNKS):
        copies = []
        for k, to in order:
            copy = remote(send_buf.at[h, to], recv_buf.at[h, g], ws.at[h, k], wr.at[h, k], wide=to)
            copy.start()
            copies.append(copy)
        wide_copies.append(copies)
        sent.extend(copies)
    loads[3].wait()
    loads[4].wait()
    table = table_ref[...]
    height = table.shape[0]
    pieces = []
    shift = 0
    while ((height * 128 - 1) >> shift) > 0:
        pieces.append(((table >> shift) & 255).astype(jnp.float32).astype(jnp.bfloat16))
        shift += 8
    n_docs = docs_ref.shape[0]
    hi_iota = lax.broadcasted_iota(jnp.int32, (height, n_docs), 0)
    lo_iota = lax.broadcasted_iota(jnp.int32, (128, n_docs), 0)
    for p in range(pos):
        ids = pos_ref[p:p + 1, :]
        hot = jnp.where(hi_iota == ids // 128, 1.0, 0.0).astype(jnp.bfloat16)
        low = lo_iota == ids % 128
        total = jnp.zeros((1, n_docs), jnp.float32)
        for i, piece in enumerate(pieces):
            rows = lax.dot_general(piece, hot, (((0,), (0,)), ((), ())), preferred_element_type=jnp.float32)
            total = total + jnp.sum(jnp.where(low, rows, 0.0), axis=0, keepdims=True) * float(1 << (8 * i))
        slot_buf[p:p + 1, :] = total.astype(jnp.int32)

    slot_copies = []
    for k, to in order:
        copy = remote(slot_buf, slot_recv.at[g], ss.at[k], sr.at[k], wide=to)
        copy.start()
        slot_copies.append(copy)
    sent.extend(slot_copies)
    slot_recv[g] = slot_buf[...]
    for h in range(CHUNKS):
        recv_buf[h, g] = send_buf[h, g]

    def take_wide(h):
        for copy in wide_copies[h]:
            copy.wait_recv()
        for j in range(F):
            pick = recv_buf[h, 0]
            for s in range(1, G):
                pick = jnp.where(owner[j] == s, recv_buf[h, s], pick)
            xb[h, j, n] = pick

    def take_slots():
        for copy in slot_copies:
            copy.wait_recv()
        for j in range(F):
            spick = slot_recv[0]
            for s in range(1, G):
                spick = jnp.where(owner[j] == s, slot_recv[s], spick)
            chosen = spick[:, :DBLK]
            for b in range(1, own):
                chosen = jnp.where(blocks[j] % own == b, spick[:, b * DBLK:(b + 1) * DBLK], chosen)
            for h in range(CHUNKS):
                slots[h, :, j * half:(j + 1) * half] = chosen[:, h * half:(h + 1) * half]

    def gather_send(h):
        piece = xb.at[h, :, n]
        across = []
        for k in range(1, outer):
            copy = remote(piece, piece, bs.at[h, k], br.at[h, k], narrow=lax.rem(n + 2 * k, N))
            copy.start()
            across.append(copy)
        near = remote(piece, piece, as_.at[h], ar.at[h], narrow=partner)
        near.start()
        sent.extend(across + [near])
        return across, near

    def gather_forward(h, across):
        passed = []
        for k in range(1, outer):
            across[k - 1].wait_recv()
            piece = xb.at[h, :, lax.rem(n + N - 2 * k, N)]
            copy = remote(piece, piece, cs.at[h, k], cr.at[h, k], narrow=partner)
            copy.start()
            passed.append(copy)
        sent.extend(passed)
        return passed

    loads[2].wait()
    pair_labels = pl_ref[...]
    me = g * N + n
    label_base = me * labels
    step = 4 if F % 4 == 0 else 2 if F % 2 == 0 else 1
    width = step * half
    span = F * half
    lane_block = lax.broadcasted_iota(jnp.int32, (1, width), 1) // half
    live = [[
        largest(jnp.where((pair_docs == blocks[j]) & (pair_labels == c) & (device_of == me), 1.0, 0.0))
        for c in range(lb_dev)] for j in range(F)]

    def compute(h):
        for j0 in range(0, F, step):
            x = xb[h, j0:j0 + step].reshape(width, D)
            at = h * span + j0 * half
            chosen_slots = slots[h, :, j0 * half:j0 * half + width]
            for c in range(lb_dev):
                weight = live[j0][c]
                for jj in range(1, step):
                    weight = jnp.where(lane_block == jj, live[j0 + jj][c], weight)
                logits = lax.dot_general(
                    w_ref[c * LBLK:(c + 1) * LBLK, :], x, (((1,), (1,)), ((), ())),
                    preferred_element_type=jnp.float32) * scale
                ids = lax.broadcasted_iota(jnp.int32, (LBLK, width), 0) + (label_base + c * LBLK)
                hit = ids == chosen_slots[0:1, :]
                for p in range(1, pos):
                    hit = hit | (ids == chosen_slots[p:p + 1, :])
                target = jnp.where(hit, 1.0, 0.0)
                grad = ((jax.nn.sigmoid(logits) - target) * scale * weight).astype(jnp.bfloat16)
                grad_ref[c * LBLK:(c + 1) * LBLK, at:at + width] = grad
            gx = lax.dot_general(
                w_ref[...], grad_ref[:, at:at + width], (((0,), (0,)), ((), ())),
                preferred_element_type=jnp.float32)
            gq[h, :, :, j0 * half:j0 * half + width] = gx.astype(jnp.bfloat16).reshape(N, feat, width)

    def reduce_first(h):
        copies = []
        for k in reversed(range(outer)):
            copy = remote(gq.at[h, lax.rem(partner + 2 * k, N)], rs1.at[h, k], ds_.at[h, k], dr.at[h, k],
                          narrow=partner)
            copy.start()
            copies.append(copy)
        sent.extend(copies)
        return copies[::-1]

    def reduce_second(h, first):
        copies = []
        for k in range(1, outer):
            first[k].wait_recv()
            to = lax.rem(n + 2 * k, N)
            mid[h, k] = (gq[h, to].astype(jnp.float32) + rs1[h, k].astype(jnp.float32)).astype(jnp.bfloat16)
            copy = remote(mid.at[h, k], rs2.at[h, k], es.at[h, k], er.at[h, k], narrow=to)
            copy.start()
            copies.append(copy)
        sent.extend(copies)
        return copies

    def send_back(h, first, second):
        first[0].wait_recv()
        total = gq[h, n].astype(jnp.float32) + rs1[h, 0].astype(jnp.float32)
        for k in range(1, outer):
            second[k - 1].wait_recv()
            total = total + rs2[h, k].astype(jnp.float32)
        total = total.astype(jnp.bfloat16)
        rows = feat // CHUNKS
        packed = [
            jnp.concatenate(
                [total[i * rows:(i + 1) * rows, j * half:(j + 1) * half] for i in range(CHUNKS)], axis=1)
            for j in range(F)]
        for d in range(G):
            back = jnp.zeros((rows, DBLK), jnp.bfloat16)
            for j in range(F):
                back = jnp.where(owner[j] == d, packed[j], back)
            ret[h, d] = back
        copies = []
        for k, to in order:
            copy = remote(ret.at[h, to], ret_recv.at[h, g], fs.at[h, k], fr.at[h, k], wide=to)
            copy.start()
            copies.append(copy)
        ret_recv[h, g] = ret[h, g]
        sent.extend(copies)
        return copies

    def update(c):
        rows = slice(c * LBLK, (c + 1) * LBLK)
        grad_w = jnp.dot(
            grad_ref[rows, :], xb[...].reshape(CHUNKS * span, D), preferred_element_type=jnp.float32)
        momentum = decay_rate * new_m_ref[rows, :] + grad_w
        new_m_ref[rows, :] = momentum
        new_w_ref[rows, :] = (w_ref[rows, :].astype(jnp.float32) - step_rate * momentum).astype(jnp.bfloat16)

    def take_back(h, copies):
        for copy in copies:
            copy.wait_recv()
        rows = feat // CHUNKS
        for b in range(own):
            total = jnp.zeros((rows, DBLK), jnp.float32)
            for s in range(G):
                total = total + jnp.where(asked_buf[s:s + 1, :] == b, ret_recv[h, s].astype(jnp.float32), 0.0)
            for i in range(CHUNKS):
                out_ref[i * rows:(i + 1) * rows, b * DBLK + h * half:b * DBLK + (h + 1) * half] = (
                    total[:, i * half:(i + 1) * half])

    gathers = []
    for h in range(CHUNKS):
        take_wide(h)
        across, near = gather_send(h)
        if h + 1 < CHUNKS:
            passed = gather_forward(h, across)
        else:
            passed = None
        gathers.append([across, near, passed])
    loads[5].wait()
    take_slots()

    backs = []
    pending = None
    for h in range(CHUNKS):
        across, near, passed = gathers[h]
        if passed is None:
            passed = gather_forward(h, across)
        if pending is not None:
            pending = pending + (reduce_second(pending[0], pending[1]),)
        near.wait_recv()
        for copy in passed:
            copy.wait_recv()
        compute(h)
        first = reduce_first(h)
        if pending is not None:
            backs.append(send_back(*pending))
        pending = (h, first)
    loads[6].wait()
    update(0)
    pending = pending + (reduce_second(*pending),)
    for c in range(1, lb_dev - 1):
        update(c)
    backs.append(send_back(*pending))
    for c in range(max(1, lb_dev - 1), lb_dev):
        update(c)
    for h in range(CHUNKS):
        take_back(h, backs[h])

    for copy in sent:
        copy.wait_send()


def store_kernel(a_ref, b_ref, c_ref, a_out, b_out, c_out, sem):
    stores = [
        pltpu.make_async_copy(src, dst, sem.at[i])
        for i, (src, dst) in enumerate(((b_ref, b_out), (a_ref, a_out), (c_ref, c_out)))]
    for store in stores:
        store.start()
    for store in stores:
        store.wait()


def per_device(documents, weights, momentum, positives, relocation, pair_docs, pair_labels):
    G = lax.axis_size("wide")
    N = lax.axis_size("narrow")
    labels, D = weights.shape
    lb_dev = labels // LBLK
    F = pair_docs.shape[1] // lb_dev
    docs = documents.shape[0]
    feat = D // N
    half = DBLK // CHUNKS
    part = half // N
    pos = positives.shape[1]
    outer = N // 2
    span = F * half
    table = relocation.reshape(-1, 128)
    pair_docs = pair_docs.T
    pair_labels = pair_labels.T
    positives = positives.T
    vmem = pl.BlockSpec(memory_space=pltpu.VMEM)
    hbm = pl.BlockSpec(memory_space=pltpu.HBM)
    dma = pltpu.SemaphoreType.DMA
    bf16 = jnp.bfloat16
    f32 = jnp.float32
    C = CHUNKS
    new_weights, new_momentum, out = pl.pallas_call(
        functools.partial(kernel, G, N, F),
        out_shape=(
            jax.ShapeDtypeStruct((labels, D), bf16),
            jax.ShapeDtypeStruct((labels, D), f32),
            jax.ShapeDtypeStruct((feat, docs), f32),
        ),
        in_specs=[hbm] * 7,
        out_specs=(vmem, vmem, vmem),
        scratch_shapes=[
            pltpu.VMEM(documents.shape, bf16),
            pltpu.VMEM(positives.shape, jnp.int32),
            pltpu.VMEM(table.shape, jnp.int32),
            pltpu.VMEM(pair_docs.shape, jnp.int32),
            pltpu.VMEM(pair_labels.shape, jnp.int32),
            pltpu.VMEM((labels, D), bf16),
            pltpu.VMEM((C, G, part, D), bf16),
            pltpu.VMEM((C, G, part, D), bf16),
            pltpu.VMEM((pos, docs), jnp.int32),
            pltpu.VMEM((G, pos, docs), jnp.int32),
            pltpu.VMEM((C, F, N, part, D), bf16),
            pltpu.VMEM((C, pos, span), jnp.int32),
            pltpu.VMEM((G, 128), jnp.int32),
            pltpu.VMEM((labels, C * span), bf16),
            pltpu.VMEM((C, N, feat, span), bf16),
            pltpu.VMEM((C, outer, feat, span), bf16),
            pltpu.VMEM((C, outer, feat, span), bf16),
            pltpu.VMEM((C, outer, feat, span), bf16),
            pltpu.VMEM((C, G, feat // C, DBLK), bf16),
            pltpu.VMEM((C, G, feat // C, DBLK), bf16),
            dma((7,)),
            dma((C, G)), dma((C, G)), dma((G,)), dma((G,)),
            dma((C,)), dma((C,)), dma((C, outer)), dma((C, outer)), dma((C, outer)), dma((C, outer)),
            dma((C, outer)), dma((C, outer)), dma((C, outer)), dma((C, outer)),
            dma((C, G)), dma((C, G)),
        ],
        compiler_params=pltpu.CompilerParams(
            collective_id=0, has_side_effects=True, vmem_limit_bytes=48 << 20),
    )(*(pltpu.with_memory_space_constraint(x, pltpu.HBM) for x in (
        documents, positives, table, pair_docs, pair_labels, weights, momentum)))
    results = (new_weights, new_momentum, out)
    new_weights, new_momentum, out = pl.pallas_call(
        store_kernel,
        out_shape=[jax.ShapeDtypeStruct(x.shape, x.dtype) for x in results],
        in_specs=[vmem] * 3,
        out_specs=[hbm] * 3,
        scratch_shapes=[dma((3,))],
        compiler_params=pltpu.CompilerParams(vmem_limit_bytes=8 << 20),
    )(*results)
    return (new_weights, new_momentum, out.T)


def solution(mesh):
    in_specs = (
        P("wide", None),
        P(("wide", "narrow"), None),
        P(("wide", "narrow"), None),
        P("wide", None),
        P(),
        P(),
        P(),
    )
    out_specs = (P(("wide", "narrow"), None), P(("wide", "narrow"), None), P("wide", "narrow"))
    return jax.shard_map(
        per_device, mesh=mesh, in_specs=in_specs, out_specs=out_specs, check_vma=False
    )
```
